256 devices in a mesh: req: 4 (over z_lo, core), exp: 64 (over y, x, z_hi).
Axes of the slice: x: 4, y: 4, z: 8 (z_hi: 4, z_lo: 2; z = z_hi * 2 + z_lo), core: 2. Of those that a mesh axis runs over, the one named last changes fastest.
Arguments:
- residual: bfloat16 [8192, 2048], P('exp'), may hold values from -6 to 6
- queries: bfloat16 [8192, 2048], P('exp', 'req'), may hold values from -128 to 128, as said below
- prefix_kv: bfloat16 [4, 16384, 256], P('req', 'exp'), may hold values from -4.5 to 4.5
- suffix_kv: bfloat16 [8192, 4, 256], P('exp', 'req'), may hold values from -6 to 6
- suffix_lengths: int32 [64, 4], P('exp'), may hold values from 1 to 96, 128 in all within a row
- out_proj: bfloat16 [2048, 2048], P('req'), may hold values from -0.5 to 0.5
- norm_gain: bfloat16 [2048], replicated, may hold values from 0.099609375 to 1.8984375
- routes: int32 [8192, 6], P('exp'), may hold values from 0 to 63, all different within a row; in each aligned block of 128 rows (0 to 127, 128 to 255, ...) at most 24 rows name the same one
- route_weights: float32 [8192, 6], P('exp'), may hold values from 0.1 to 0.5
- expert_gate: bfloat16 [64, 2048, 1408], P('exp', None, 'req'), may hold values from -0.125 to 0.125
- expert_up: bfloat16 [64, 2048, 1408], P('exp', None, 'req'), may hold values from -0.125 to 0.125
- expert_down: bfloat16 [64, 1408, 2048], P('exp', 'req'), may hold values from -0.15625 to 0.15625
- shared_gate: bfloat16 [2048, 1408], P(None, 'req'), may hold values from -0.125 to 0.125
- shared_up: bfloat16 [2048, 1408], P(None, 'req'), may hold values from -0.125 to 0.125
- shared_down: bfloat16 [1408, 2048], P('req'), may hold values from -0.15625 to 0.15625
Outputs:
- layer_out: bfloat16 [8192, 2048], P('exp')
The draws below stay inside these ranges and needn't reach their ends.
Inputs may be any that keep to these rules, and one draw needn't show every extreme that they name: In the hidden draw some queries are strong multiples of prefix keys. `suffix_lengths`: each row (the requests of one index of exp) sums to 128, and in every row one request has exactly 96 tokens. `routes`: the 6 experts of a token are different. Among the 128 tokens of one index of exp no expert is picked more than 24 times, and in every draw some expert is picked exactly 24 times by the tokens of some index of exp.
All inputs are finite; a program needn't handle non-finite values.
Results may differ from the reference program's by a relative error of at most 0.015.
Values may be sent and summed in bfloat16 or wider, within the bound.
A program may use at most 128 MiB of HBM per device.

```python
import math
import jax
import jax.numpy as jnp
import numpy as np
from jax import lax

D = 2048
H = 16
KVH = 4
HD = 128
FF_EXP = 1408
TOP = 6
SHARED = 1408
TOK_DEV = 128
REQS_DEV = 4
EXPERTS = 64
LONGEST = 96
CAP = 24
TOKENS = 8192
PREFIX = 16384
N_REQ = 4
N_EXP = 64


def prefix_table(key):
    sample_base = jax.random.normal(jax.random.fold_in(key, 11), (KVH, PREFIX, 2 * HD), jnp.float32)
    sample_base = jnp.clip(sample_base, -4.5, 4.5)
    return sample_base


def draw_prefix_kv(key, part):
    return prefix_table(key).astype(jnp.bfloat16)


def draw_queries(key, part):
    sample_base = 2.5 * jax.random.normal(jax.random.fold_in(key, 12), (TOKENS, H * HD), jnp.float32)
    return jnp.clip(sample_base, -128.0, 128.0).astype(jnp.bfloat16)


def shard_levels(key, shape, shards, least, high):
    level = 1.0
    for dim, parts in shards:
        heights = jax.random.uniform(jax.random.fold_in(jax.random.fold_in(key, 6), dim), (parts,), jnp.float32, least / len(shards), high / len(shards))
        level = level * jnp.repeat(jnp.exp(heights), shape[dim] // parts).reshape((-1,) + (1,) * (len(shape) - 1 - dim))
    return level


def length_profile(amount, total, bound, skew):
    portions = [(1 << 20) // math.isqrt(rank ** skew) + 1 for rank in range(2, amount + 1)]
    surplus, holding = total - bound - (amount - 1), [1] * (amount - 1)
    while surplus > 0:
        candidates = [i for i in range(amount - 1) if holding[i] < bound]
        mass, left = sum([portions[i] for i in candidates]), surplus
        for i in candidates:
            extra = min(bound - holding[i], max(1, left * portions[i] // mass), surplus)
            holding[i] = holding[i] + extra
            surplus = surplus - extra
    return np.array([bound] + holding)


def uneven_parts(own_key, count, total, limit, skew):
    if count == 2:
        one = jax.random.randint(own_key, (), max(1, total - limit), min(limit, total - 1) + 1)
        return jnp.stack([one, total - one])
    tallies = jnp.asarray(length_profile(count, total, limit, skew), jnp.int32)
    twos = (count - 1) // 2
    donor, receiver = tallies[1:1 + 2 * twos:2], tallies[2:2 + 2 * twos:2]
    room = jnp.minimum(donor - 1, limit - receiver)
    shifted = jax.random.randint(jax.random.fold_in(own_key, 1), (twos,), 0, 1 << 20) % (room + 1)
    tallies = tallies.at[1:1 + 2 * twos:2].set(donor - shifted).at[2:2 + 2 * twos:2].set(receiver + shifted)
    return tallies[jax.random.permutation(jax.random.fold_in(own_key, 2), count)]


def routed_block(rng, own, number, rows, amount, top, reach, lean):
    order = jax.random.permutation(rng, amount)
    crowded, ordinary = portions_of(amount, rows * top, reach, lean, True), portions_of(amount, rows * top, reach, lean, False)
    places = jnp.arange(amount)

    def named(lengths, rotation):
        used = int((lengths > 0).sum())
        fixed = max(1, used // 4)
        shifted = fixed + (places - fixed + rotation * (used - fixed)) % max(1, amount - fixed)
        return jnp.zeros((amount,), jnp.int32).at[order[jnp.where(places < fixed, places, shifted)]].set(jnp.asarray(lengths, jnp.int32))

    lengths = jnp.where(number % 4 == 0, named(crowded, number // 4), named(ordinary, number - number // 4 - 1))
    mixed = jax.random.permutation(jax.random.fold_in(own, 3), amount)
    giver, receiver = mixed[0:amount // 2 * 2:2], mixed[1:amount // 2 * 2:2]
    slack = jnp.minimum(lengths[giver] - 1, reach - lengths[receiver]) // 2
    slack = jnp.where((giver == order[0]) | (receiver == order[0]) | (lengths[receiver] == 0), 0, jnp.maximum(slack, 0))
    shifted = jax.random.randint(jax.random.fold_in(own, 4), (amount // 2,), 0, 1 << 20) % (slack + 1)
    lengths = lengths.at[giver].add(-shifted).at[receiver].add(shifted)
    items = jnp.searchsorted(jnp.cumsum(lengths), jnp.arange(rows * top), side="right").astype(jnp.int32)
    listing = items.reshape(top, rows).T
    listing = listing[jax.random.permutation(jax.random.fold_in(own, 1), rows)]
    rotation = jax.random.randint(jax.random.fold_in(own, 2), (rows, 1), 0, top)
    return jnp.take_along_axis(listing, (jnp.arange(top)[None, :] + rotation) % top, axis=1)


def portions_of(count, total, limit, slope, full):
    portions = [(1 << 20) // math.isqrt(standing ** slope) + 1 for standing in range(1, count + 1)]
    largest = limit if full else min(limit, max(-(-total // count), total * portions[0] // sum(portions)))
    least = 1 if total - largest >= count - 1 else 0
    given, surplus = [largest] + [least] * (count - 1), total - largest - least * (count - 1)
    while surplus > 0:
        movable = [i for i in range(1, count) if given[i] < largest] or [i for i in range(1, count) if given[i] < limit]
        whole, left = sum([portions[i] for i in movable]), surplus
        for i in movable:
            extra = min(limit - given[i], max(1, left * portions[i] // whole), surplus)
            given[i] = given[i] + extra
            surplus = surplus - extra
    return np.array(given)


def bell_draw(own_key, extent, deviation, bound, pieces=(), kind=jnp.bfloat16):
    gain = shard_levels(own_key, extent, pieces, -0.22, 0.18) if pieces else 1.0
    values = jax.random.normal(own_key, extent, jnp.float32) * deviation * gain
    return jnp.minimum(jnp.maximum(values, -bound), bound).astype(kind)


def setup_inputs(seed: int = 0) -> dict:
    streams_of = jax.random.split(jax.random.key(seed), 16)
    residual = bell_draw(streams_of[0], (TOKENS, D), 1.0, 6.0, ((0, 64),))
    queries = draw_queries(jax.random.fold_in(streams_of[15], 71), 0)
    prefix_kv = draw_prefix_kv(jax.random.fold_in(streams_of[15], 71), 0)
    suffix_kv = bell_draw(streams_of[3], (TOKENS, KVH, 2 * HD), 1.0, 6.0, ((0, 64), (1, 4)))
    suffix_lengths = jax.vmap(lambda own: uneven_parts(own, REQS_DEV, TOK_DEV, LONGEST, 2))(jax.random.split(streams_of[4], N_EXP)).reshape((N_EXP, REQS_DEV)).astype(jnp.int32)
    out_proj = bell_draw(streams_of[5], (H * HD, D), HD ** -0.5, 0.5, ((0, 4),))
    norm_gain = jnp.clip(1.0 + 0.18 * jax.random.normal(streams_of[6], (D,), jnp.float32), 0.099609375, 1.8984375).astype(jnp.bfloat16)
    routes_keys = jax.random.split(jax.random.fold_in(streams_of[7], 1), TOKENS // TOK_DEV)
    routes_turns = jax.random.permutation(jax.random.fold_in(streams_of[7], 3), TOKENS // TOK_DEV)
    routes = jax.vmap(lambda own, number: routed_block(jax.random.fold_in(streams_of[7], 2), own, number, TOK_DEV, EXPERTS, TOP, CAP, 2))(routes_keys, routes_turns).reshape((TOKENS, TOP))
    route_weights = jnp.clip(0.1 + 0.4 * jax.random.uniform(streams_of[8], (TOKENS, TOP), jnp.float32) ** shard_levels(streams_of[8], (TOKENS, TOP), ((0, 64),), -0.2, 0.2), 0.1, 0.5)
    expert_gate = bell_draw(streams_of[9], (EXPERTS, D, FF_EXP), D ** -0.5, 0.125, ((0, 64), (2, 4)))
    expert_up = bell_draw(streams_of[10], (EXPERTS, D, FF_EXP), D ** -0.5, 0.125, ((0, 64), (2, 4)))
    expert_down = bell_draw(streams_of[11], (EXPERTS, FF_EXP, D), FF_EXP ** -0.5, 0.15625, ((0, 64), (1, 4)))
    shared_gate = bell_draw(streams_of[12], (D, SHARED), D ** -0.5, 0.125, ((1, 4),))
    shared_up = bell_draw(streams_of[13], (D, SHARED), D ** -0.5, 0.125, ((1, 4),))
    shared_down = bell_draw(streams_of[14], (SHARED, D), SHARED ** -0.5, 0.15625, ((0, 4),))
    return {"residual": residual, "queries": queries, "prefix_kv": prefix_kv, "suffix_kv": suffix_kv, "suffix_lengths": suffix_lengths, "out_proj": out_proj, "norm_gain": norm_gain, "routes": routes, "route_weights": route_weights, "expert_gate": expert_gate, "expert_up": expert_up, "expert_down": expert_down, "shared_gate": shared_gate, "shared_up": shared_up, "shared_down": shared_down}


neg_big = -1e+30
norm_eps = 1e-06

def reference(residual, queries, prefix_kv, suffix_kv, suffix_lengths, out_proj, norm_gain, routes, route_weights, expert_gate, expert_up, expert_down, shared_gate, shared_up, shared_down):
    group_size = H // KVH
    scaling = 1.0 / HD ** 0.5
    prefix_keys = prefix_kv[:, :, :HD].astype(jnp.float32)
    prefix_vals = prefix_kv[:, :, HD:].astype(jnp.float32)

    def column_attention(packed):
        query_col, suffix_col, length_col = packed
        query_heads = query_col.astype(jnp.float32).reshape(TOK_DEV, KVH, group_size, HD)
        suffix_keys = jnp.transpose(suffix_col[:, :, :HD].astype(jnp.float32), (1, 0, 2))
        suffix_vals = jnp.transpose(suffix_col[:, :, HD:].astype(jnp.float32), (1, 0, 2))
        keys_all = jnp.concatenate([prefix_keys, suffix_keys], axis=1)
        vals_all = jnp.concatenate([prefix_vals, suffix_vals], axis=1)
        scores = jnp.einsum('tgjd,gkd->gjtk', query_heads, keys_all) * scaling
        request_ends = jnp.cumsum(length_col)
        positions = jnp.arange(TOK_DEV, dtype=jnp.int32)
        request_ids = lax.optimization_barrier(jnp.sum((positions[:, None] >= request_ends[None, :]).astype(jnp.int32), axis=1))
        allowed = (request_ids[:, None] == request_ids[None, :]) & (positions[None, :] <= positions[:, None])
        allowed_all = jnp.concatenate([jnp.ones((TOK_DEV, PREFIX), dtype=bool), allowed], axis=1)
        scores = jnp.where(allowed_all[None, None], scores, neg_big)
        row_max = lax.optimization_barrier(jnp.max(scores, axis=-1, keepdims=True))
        exp_scores = jnp.exp(scores - row_max)
        row_sum = lax.optimization_barrier(jnp.sum(exp_scores, axis=-1))
        exp_weights = lax.optimization_barrier(exp_scores.astype(jnp.bfloat16)).astype(jnp.float32)
        attended = jnp.einsum('gjtk,gkd->tgjd', exp_weights, vals_all)
        attended = attended / jnp.transpose(row_sum, (2, 0, 1))[..., None]
        return attended.reshape(TOK_DEV, H * HD).astype(jnp.bfloat16)
    query_cols = queries.reshape(N_EXP, TOK_DEV, H * HD)
    suffix_cols = suffix_kv.reshape(N_EXP, TOK_DEV, KVH, 2 * HD)
    attention = lax.map(column_attention, (query_cols, suffix_cols, suffix_lengths)).reshape(TOKENS, H * HD)
    attn_out = jnp.dot(attention, out_proj, preferred_element_type=jnp.float32)
    hidden_state = (residual.astype(jnp.float32) + attn_out).astype(jnp.bfloat16)
    hidden_float = hidden_state.astype(jnp.float32)
    mean_square = lax.optimization_barrier(jnp.mean(hidden_float * hidden_float, axis=-1, keepdims=True))
    normed = (hidden_float * lax.rsqrt(mean_square + norm_eps) * norm_gain.astype(jnp.float32)).astype(jnp.bfloat16)
    shared_gate_act = jnp.dot(normed, shared_gate, preferred_element_type=jnp.float32)
    shared_up_act = jnp.dot(normed, shared_up, preferred_element_type=jnp.float32)
    shared_hidden = (jax.nn.silu(shared_gate_act) * shared_up_act).astype(jnp.bfloat16)
    shared_out = jnp.dot(shared_hidden, shared_down, preferred_element_type=jnp.float32)
    pick_ids = routes.reshape(-1).astype(jnp.int32)
    pick_tokens = (jnp.arange(TOKENS * TOP, dtype=jnp.int32) // TOP).astype(jnp.int32)
    pick_weights = route_weights.reshape(-1).astype(jnp.float32)
    one_hot = (pick_ids[:, None] == jnp.arange(EXPERTS, dtype=jnp.int32)[None, :]).astype(jnp.int32)
    pick_ranks = lax.optimization_barrier(jnp.sum((jnp.cumsum(one_hot, axis=0) - one_hot) * one_hot, axis=1)).astype(jnp.int32)
    slots_per = N_EXP * CAP
    token_table = jnp.full((EXPERTS, slots_per), TOKENS, dtype=jnp.int32).at[pick_ids, pick_ranks].set(pick_tokens)
    weight_table = jnp.zeros((EXPERTS, slots_per), jnp.float32).at[pick_ids, pick_ranks].set(pick_weights)
    normed_pad = jnp.concatenate([normed, jnp.zeros((1, D), normed.dtype)], axis=0)
    block_len = FF_EXP // N_REQ

    def expert_step(carried, packed):
        gate_w, up_w, down_w, token_ids, weight_ids = packed
        source_rows = normed_pad[token_ids]
        gate_act = jnp.dot(source_rows, gate_w, preferred_element_type=jnp.float32)
        up_act = jnp.dot(source_rows, up_w, preferred_element_type=jnp.float32)
        expert_hidden = (jax.nn.silu(gate_act) * up_act).astype(jnp.bfloat16)
        summed = jnp.zeros((slots_per, D), jnp.float32)
        for block_id in range(N_REQ):
            slice_out = jnp.dot(expert_hidden[:, block_id * block_len:(block_id + 1) * block_len], down_w[block_id * block_len:(block_id + 1) * block_len], preferred_element_type=jnp.float32).astype(jnp.bfloat16)
            summed = summed + slice_out.astype(jnp.float32)
        return (carried.at[token_ids].add(summed * weight_ids[:, None]), None)
    routed, unused = lax.scan(expert_step, jnp.zeros((TOKENS + 1, D), jnp.float32), (expert_gate, expert_up, expert_down, token_table, weight_table))
    return (hidden_float + shared_out + routed[:TOKENS]).astype(jnp.bfloat16)
```

```python
import math

import jax
import jax.numpy as jnp
from jax import lax
from jax.experimental import pallas as pl
from jax.experimental.pallas import tpu as pltpu
from jax.sharding import PartitionSpec as P

HD = 128
TOP = 6
CAP = 24

neg_big = -1e30
norm_eps = 1e-06

CORE_SWAP = [(0, 1), (1, 0), (2, 3), (3, 2)]
CHIP_SWAP = [(0, 2), (2, 0), (1, 3), (3, 1)]

KEY_BLOCK = 2048
KEY_CHUNK = 512


def attend_kernel(q_ref, kv_ref, suffix_ref, mask_ref, out_ref, q_rows, top, total, acc):
    step = pl.program_id(0)
    tokens = q_ref.shape[0]
    heads = q_ref.shape[1] // HD
    scale = math.log2(math.e) / math.sqrt(HD)

    def score(keys):
        return lax.dot_general(
            keys, q_rows[...], (((1,), (1,)), ((), ())), preferred_element_type=jnp.float32
        ) * scale

    def weigh(values, weights):
        return lax.dot_general(
            values,
            weights.astype(jnp.bfloat16),
            (((0,), (0,)), ((), ())),
            preferred_element_type=jnp.float32,
        )

    @pl.when(step == 0)
    def _():
        for h in range(heads):
            q_rows[h * tokens : (h + 1) * tokens, :] = q_ref[:, h * HD : (h + 1) * HD]
        mask = jnp.concatenate([mask_ref[...]] * heads, axis=1)
        scores = jnp.where(mask > 0.5, score(suffix_ref[:, :HD]), neg_big)
        first = jnp.max(scores, axis=0, keepdims=True)
        weights = jnp.exp2(scores - first)
        top[...] = first
        total[...] = jnp.sum(weights, axis=0, keepdims=True)
        acc[...] = weigh(suffix_ref[:, HD:], weights)

    running_top, running_total, running_acc = top[...], total[...], acc[...]
    for c in range(KEY_BLOCK // KEY_CHUNK):
        rows = slice(c * KEY_CHUNK, (c + 1) * KEY_CHUNK)
        scores = score(kv_ref[0, rows, :HD])
        new_top = jnp.maximum(running_top, jnp.max(scores, axis=0, keepdims=True))
        factor = jnp.exp2(running_top - new_top)
        weights = jnp.exp2(scores - new_top)
        running_total = running_total * factor + jnp.sum(weights, axis=0, keepdims=True)
        running_acc = running_acc * factor + weigh(kv_ref[0, rows, HD:], weights)
        running_top = new_top
    top[...], total[...], acc[...] = running_top, running_total, running_acc

    @pl.when(step == pl.num_programs(0) - 1)
    def _():
        done = running_acc / running_total
        for h in range(heads):
            out_ref[:, h * HD : (h + 1) * HD] = done[:, h * tokens : (h + 1) * tokens].T.astype(
                jnp.bfloat16
            )


def attend(queries, prefix, suffix, mask):
    tokens, width = queries.shape
    columns = tokens * (width // HD)
    steps = prefix.shape[1] // KEY_BLOCK
    return pl.pallas_call(
        attend_kernel,
        grid=(steps,),
        out_shape=jax.ShapeDtypeStruct((tokens, width), jnp.bfloat16),
        in_specs=[
            pl.BlockSpec((tokens, width), lambda i: (0, 0)),
            pl.BlockSpec((1, KEY_BLOCK, 2 * HD), lambda i: (0, i, 0)),
            pl.BlockSpec(suffix.shape, lambda i: (0, 0)),
            pl.BlockSpec(mask.shape, lambda i: (0, 0)),
        ],
        out_specs=pl.BlockSpec((tokens, width), lambda i: (0, 0)),
        scratch_shapes=[
            pltpu.VMEM((columns, HD), jnp.bfloat16),
            pltpu.VMEM((1, columns), jnp.float32),
            pltpu.VMEM((1, columns), jnp.float32),
            pltpu.VMEM((HD, columns), jnp.float32),
        ],
        compiler_params=pltpu.CompilerParams(
            dimension_semantics=("arbitrary",), vmem_limit_bytes=40 * 1024 * 1024
        ),
        cost_estimate=pl.CostEstimate(
            flops=4 * columns * prefix.shape[1] * HD,
            bytes_accessed=prefix.size * 2,
            transcendentals=columns * prefix.shape[1],
        ),
        name="attend",
    )(queries, prefix, suffix, mask)


def half_sum(terms, core):
    half = terms.shape[0] // 2
    mine = lax.dynamic_slice_in_dim(terms, core * half, half, 0)
    other = lax.dynamic_slice_in_dim(terms, (1 - core) * half, half, 0)
    came = lax.ppermute(other, "req", CORE_SWAP)
    chip = lax.optimization_barrier(
        (mine.astype(jnp.float32) + came.astype(jnp.float32)).astype(jnp.bfloat16)
    )
    across = lax.ppermute(chip, "req", CHIP_SWAP)
    return chip.astype(jnp.float32) + across.astype(jnp.float32)


def whole_rows(half, core):
    half = lax.optimization_barrier(half)
    other = lax.ppermute(half, "req", CORE_SWAP)
    low = jnp.where(core == 0, half, other)
    high = jnp.where(core == 0, other, half)
    return jnp.concatenate([low, high], axis=0)


def on_device(
    residual,
    queries,
    prefix_kv,
    suffix_kv,
    suffix_lengths,
    out_proj,
    norm_gain,
    routes,
    route_weights,
    expert_gate,
    expert_up,
    expert_down,
    shared_gate,
    shared_up,
    shared_down,
):
    tokens_here, feat_width = residual.shape
    half = tokens_here // 2
    exp_count = lax.axis_size("exp")
    req_count = lax.axis_size("req")
    me = lax.axis_index("req")
    core = me % 2
    slots = CAP // req_count
    rows_here = exp_count * slots

    portion = lax.all_gather(prefix_kv, "exp", axis=1, tiled=True)

    own = (expert_gate[0], expert_up[0], expert_down[0])
    beside = tuple(lax.ppermute(w, "req", CORE_SWAP) for w in own)
    across = tuple(lax.ppermute(w, "req", CHIP_SWAP) for w in own)
    far = tuple(lax.ppermute(w, "req", CORE_SWAP) for w in across)

    request_ends = jnp.cumsum(suffix_lengths[0])
    positions = jnp.arange(tokens_here, dtype=jnp.int32)
    request_ids = jnp.sum((positions[:, None] >= request_ends[None, :]).astype(jnp.int32), axis=1)
    allowed = (request_ids[:, None] == request_ids[None, :]) & (
        positions[:, None] <= positions[None, :]
    )
    attention = attend(queries, portion, suffix_kv[:, 0, :], allowed.astype(jnp.float32))

    attn_terms = jnp.dot(attention, out_proj, preferred_element_type=jnp.float32)
    attn_half = half_sum(attn_terms.astype(jnp.bfloat16), core)
    residual_half = lax.dynamic_slice_in_dim(residual, core * half, half, 0)
    hidden_half = lax.optimization_barrier(
        (residual_half.astype(jnp.float32) + attn_half).astype(jnp.bfloat16)
    )
    hidden_float = hidden_half.astype(jnp.float32)
    mean_square = jnp.mean(hidden_float * hidden_float, axis=-1, keepdims=True)
    normed = whole_rows(
        (
            hidden_float * lax.rsqrt(mean_square + norm_eps) * norm_gain.astype(jnp.float32)
        ).astype(jnp.bfloat16),
        core,
    )

    pick_ids = routes.reshape(-1)
    experts = jnp.arange(exp_count, dtype=jnp.int32)
    one_hot = (pick_ids[:, None] == experts[None, :]).astype(jnp.int32)
    pick_ranks = jnp.sum((jnp.cumsum(one_hot, axis=0) - one_hot) * one_hot, axis=1)
    pick_slots = jnp.where(
        pick_ranks // slots == me, pick_ids * slots + pick_ranks % slots, -1
    ).reshape(tokens_here, TOP)
    slot_ids = jnp.arange(rows_here, dtype=jnp.int32)
    chosen = pick_slots[:, :, None] == slot_ids[None, None, :]
    placement = jnp.any(chosen, axis=1).astype(jnp.bfloat16)
    mix = jnp.sum(jnp.where(chosen, route_weights[:, :, None], 0.0), axis=1)
    mix_high = lax.reduce_precision(mix, 8, 7)
    mix_low = (mix - mix_high).astype(jnp.bfloat16)
    mix_high = mix_high.astype(jnp.bfloat16)

    lanes = feat_width // HD
    buffer = lax.dot_general(
        placement, normed, (((0,), (0,)), ((), ())), preferred_element_type=jnp.float32
    ).astype(jnp.bfloat16)
    sent = lax.all_to_all(
        buffer.reshape(exp_count, slots * lanes, HD), "exp", split_axis=0, concat_axis=0, tiled=True
    )
    source_rows = sent.reshape(rows_here, feat_width)

    shared_gate_act = jnp.dot(normed, shared_gate, preferred_element_type=jnp.float32)
    shared_up_act = jnp.dot(normed, shared_up, preferred_element_type=jnp.float32)
    shared_hidden = (jax.nn.silu(shared_gate_act) * shared_up_act).astype(jnp.bfloat16)
    shared_part = jnp.dot(shared_hidden, shared_down, preferred_element_type=jnp.float32)

    expert_out = jnp.zeros((rows_here, feat_width), jnp.float32)
    for gate, up, down in (own, beside, across, far):
        gate_act = jnp.dot(source_rows, gate, preferred_element_type=jnp.float32)
        up_act = jnp.dot(source_rows, up, preferred_element_type=jnp.float32)
        expert_hidden = (jax.nn.silu(gate_act) * up_act).astype(jnp.bfloat16)
        expert_out += jnp.dot(expert_hidden, down, preferred_element_type=jnp.float32)
    returned = lax.all_to_all(
        expert_out.astype(jnp.bfloat16).reshape(exp_count, slots * lanes, HD),
        "exp",
        split_axis=0,
        concat_axis=0,
        tiled=True,
    ).reshape(rows_here, feat_width)
    routed = jnp.dot(mix_high, returned, preferred_element_type=jnp.float32) + jnp.dot(
        mix_low, returned, preferred_element_type=jnp.float32
    )
    summed = half_sum((shared_part + routed).astype(jnp.bfloat16), core)
    return whole_rows((hidden_float + summed).astype(jnp.bfloat16), core)


def solution(mesh):
    placed = (
        P("exp", None),
        P("exp", "req"),
        P("req", "exp", None),
        P("exp", "req", None),
        P("exp", None),
        P("req", None),
        P(),
        P("exp", None),
        P("exp", None),
        P("exp", None, "req"),
        P("exp", None, "req"),
        P("exp", "req", None),
        P(None, "req"),
        P(None, "req"),
        P("req", None),
    )
    return jax.shard_map(
        on_device, mesh=mesh, in_specs=placed, out_specs=P("exp", None), check_vma=False
    )
```

```python
import math

import jax
import jax.numpy as jnp
from jax import lax
from jax.experimental import pallas as pl
from jax.experimental.pallas import tpu as pltpu
from jax.sharding import PartitionSpec as P

HD = 128
TOP = 6
CAP = 24

neg_big = -1e30
norm_eps = 1e-06

CORE_SWAP = [(0, 1), (1, 0), (2, 3), (3, 2)]
CHIP_SWAP = [(0, 2), (2, 0), (1, 3), (3, 1)]

KEY_BLOCK = 2048
KEY_CHUNK = 512


def attend_kernel(q_ref, kv_ref, suffix_ref, mask_ref, out_ref, q_rows, top, total, acc):
    step = pl.program_id(0)
    tokens = q_ref.shape[0]
    heads = q_ref.shape[1] // HD
    scale = math.log2(math.e) / math.sqrt(HD)

    def score(keys):
        return lax.dot_general(
            keys, q_rows[...], (((1,), (1,)), ((), ())), preferred_element_type=jnp.float32
        ) * scale

    def weigh(values, weights):
        return lax.dot_general(
            values,
            weights.astype(jnp.bfloat16),
            (((0,), (0,)), ((), ())),
            preferred_element_type=jnp.float32,
        )

    @pl.when(step == 0)
    def _():
        for h in range(heads):
            q_rows[h * tokens : (h + 1) * tokens, :] = q_ref[:, h * HD : (h + 1) * HD]
        mask = jnp.concatenate([mask_ref[...]] * heads, axis=1)
        scores = jnp.where(mask > 0.5, score(suffix_ref[:, :HD]), neg_big)
        first = jnp.max(scores, axis=0, keepdims=True)
        weights = jnp.exp2(scores - first)
        top[...] = first
        total[...] = jnp.sum(weights, axis=0, keepdims=True)
        acc[...] = weigh(suffix_ref[:, HD:], weights)

    running_top, running_total, running_acc = top[...], total[...], acc[...]
    for c in range(KEY_BLOCK // KEY_CHUNK):
        rows = slice(c * KEY_CHUNK, (c + 1) * KEY_CHUNK)
        scores = score(kv_ref[0, rows, :HD])
        new_top = jnp.maximum(running_top, jnp.max(scores, axis=0, keepdims=True))
        factor = jnp.exp2(running_top - new_top)
        weights = jnp.exp2(scores - new_top)
        running_total = running_total * factor + jnp.sum(weights, axis=0, keepdims=True)
        running_acc = running_acc * factor + weigh(kv_ref[0, rows, HD:], weights)
        running_top = new_top
    top[...], total[...], acc[...] = running_top, running_total, running_acc

    @pl.when(step == pl.num_programs(0) - 1)
    def _():
        done = running_acc / running_total
        for h in range(heads):
            out_ref[:, h * HD : (h + 1) * HD] = done[:, h * tokens : (h + 1) * tokens].T.astype(
                jnp.bfloat16
            )


def attend(queries, prefix, suffix, mask):
    tokens, width = queries.shape
    columns = tokens * (width // HD)
    steps = prefix.shape[1] // KEY_BLOCK
    return pl.pallas_call(
        attend_kernel,
        grid=(steps,),
        out_shape=jax.ShapeDtypeStruct((tokens, width), jnp.bfloat16),
        in_specs=[
            pl.BlockSpec((tokens, width), lambda i: (0, 0)),
            pl.BlockSpec((1, KEY_BLOCK, 2 * HD), lambda i: (0, i, 0)),
            pl.BlockSpec(suffix.shape, lambda i: (0, 0)),
            pl.BlockSpec(mask.shape, lambda i: (0, 0)),
        ],
        out_specs=pl.BlockSpec((tokens, width), lambda i: (0, 0)),
        scratch_shapes=[
            pltpu.VMEM((columns, HD), jnp.bfloat16),
            pltpu.VMEM((1, columns), jnp.float32),
            pltpu.VMEM((1, columns), jnp.float32),
            pltpu.VMEM((HD, columns), jnp.float32),
        ],
        compiler_params=pltpu.CompilerParams(
            dimension_semantics=("arbitrary",), vmem_limit_bytes=40 * 1024 * 1024
        ),
        cost_estimate=pl.CostEstimate(
            flops=4 * columns * prefix.shape[1] * HD,
            bytes_accessed=prefix.size * 2,
            transcendentals=columns * prefix.shape[1],
        ),
        name="attend",
    )(queries, prefix, suffix, mask)


def half_sum(terms, core):
    half = terms.shape[0] // 2
    mine = lax.dynamic_slice_in_dim(terms, core * half, half, 0)
    other = lax.dynamic_slice_in_dim(terms, (1 - core) * half, half, 0)
    came = lax.ppermute(other, "req", CORE_SWAP)
    chip = lax.optimization_barrier(
        (mine.astype(jnp.float32) + came.astype(jnp.float32)).astype(jnp.bfloat16)
    )
    across = lax.ppermute(chip, "req", CHIP_SWAP)
    return chip.astype(jnp.float32) + across.astype(jnp.float32)


def whole_rows(half, core):
    half = lax.optimization_barrier(half)
    other = lax.ppermute(half, "req", CORE_SWAP)
    low = jnp.where(core == 0, half, other)
    high = jnp.where(core == 0, other, half)
    return jnp.concatenate([low, high], axis=0)


def on_device(
    residual,
    queries,
    prefix_kv,
    suffix_kv,
    suffix_lengths,
    out_proj,
    norm_gain,
    routes,
    route_weights,
    expert_gate,
    expert_up,
    expert_down,
    shared_gate,
    shared_up,
    shared_down,
):
    tokens_here, feat_width = residual.shape
    half = tokens_here // 2
    exp_count = lax.axis_size("exp")
    req_count = lax.axis_size("req")
    me = lax.axis_index("req")
    core = me % 2
    slots = CAP // req_count
    rows_here = exp_count * slots

    portion = lax.all_gather(prefix_kv, "exp", axis=1, tiled=True)

    own = (expert_gate[0], expert_up[0], expert_down[0])
    beside = tuple(lax.ppermute(w, "req", CORE_SWAP) for w in own)
    across = tuple(lax.ppermute(w, "req", CHIP_SWAP) for w in own)
    portion, beside, across = lax.optimization_barrier((portion, beside, across))
    far = tuple(lax.ppermute(w, "req", CORE_SWAP) for w in across)

    request_ends = jnp.cumsum(suffix_lengths[0])
    positions = jnp.arange(tokens_here, dtype=jnp.int32)
    request_ids = jnp.sum((positions[:, None] >= request_ends[None, :]).astype(jnp.int32), axis=1)
    allowed = (request_ids[:, None] == request_ids[None, :]) & (
        positions[:, None] <= positions[None, :]
    )
    attention = attend(queries, portion, suffix_kv[:, 0, :], allowed.astype(jnp.float32))
    attention, far = lax.optimization_barrier((attention, far))

    attn_terms = jnp.dot(attention, out_proj, preferred_element_type=jnp.float32)
    attn_half = half_sum(attn_terms.astype(jnp.bfloat16), core)
    residual_half = lax.dynamic_slice_in_dim(residual, core * half, half, 0)
    hidden_half = lax.optimization_barrier(
        (residual_half.astype(jnp.float32) + attn_half).astype(jnp.bfloat16)
    )
    hidden_float = hidden_half.astype(jnp.float32)
    mean_square = jnp.mean(hidden_float * hidden_float, axis=-1, keepdims=True)
    normed = whole_rows(
        (
            hidden_float * lax.rsqrt(mean_square + norm_eps) * norm_gain.astype(jnp.float32)
        ).astype(jnp.bfloat16),
        core,
    )

    pick_ids = routes.reshape(-1)
    experts = jnp.arange(exp_count, dtype=jnp.int32)
    one_hot = (pick_ids[:, None] == experts[None, :]).astype(jnp.int32)
    pick_ranks = jnp.sum((jnp.cumsum(one_hot, axis=0) - one_hot) * one_hot, axis=1)
    pick_slots = jnp.where(
        pick_ranks // slots == me, pick_ids * slots + pick_ranks % slots, -1
    ).reshape(tokens_here, TOP)
    slot_ids = jnp.arange(rows_here, dtype=jnp.int32)
    chosen = pick_slots[:, :, None] == slot_ids[None, None, :]
    placement = jnp.any(chosen, axis=1).astype(jnp.bfloat16)
    mix = jnp.sum(jnp.where(chosen, route_weights[:, :, None], 0.0), axis=1)
    mix_high = lax.reduce_precision(mix, 8, 7)
    mix_low = (mix - mix_high).astype(jnp.bfloat16)
    mix_high = mix_high.astype(jnp.bfloat16)

    lanes = feat_width // HD
    buffer = lax.dot_general(
        placement, normed, (((0,), (0,)), ((), ())), preferred_element_type=jnp.float32
    ).astype(jnp.bfloat16)
    sent = lax.all_to_all(
        buffer.reshape(exp_count, slots * lanes, HD), "exp", split_axis=0, concat_axis=0, tiled=True
    )
    source_rows = sent.reshape(rows_here, feat_width)

    shared_gate_act = jnp.dot(normed, shared_gate, preferred_element_type=jnp.float32)
    shared_up_act = jnp.dot(normed, shared_up, preferred_element_type=jnp.float32)
    shared_hidden = (jax.nn.silu(shared_gate_act) * shared_up_act).astype(jnp.bfloat16)
    shared_part = jnp.dot(shared_hidden, shared_down, preferred_element_type=jnp.float32)

    expert_out = jnp.zeros((rows_here, feat_width), jnp.float32)
    for gate, up, down in (own, beside, across, far):
        gate_act = jnp.dot(source_rows, gate, preferred_element_type=jnp.float32)
        up_act = jnp.dot(source_rows, up, preferred_element_type=jnp.float32)
        expert_hidden = (jax.nn.silu(gate_act) * up_act).astype(jnp.bfloat16)
        expert_out += jnp.dot(expert_hidden, down, preferred_element_type=jnp.float32)
    returned = lax.all_to_all(
        expert_out.astype(jnp.bfloat16).reshape(exp_count, slots * lanes, HD),
        "exp",
        split_axis=0,
        concat_axis=0,
        tiled=True,
    ).reshape(rows_here, feat_width)
    routed = jnp.dot(mix_high, returned, preferred_element_type=jnp.float32) + jnp.dot(
        mix_low, returned, preferred_element_type=jnp.float32
    )
    summed = half_sum((shared_part + routed).astype(jnp.bfloat16), core)
    return whole_rows((hidden_float + summed).astype(jnp.bfloat16), core)


def solution(mesh):
    placed = (
        P("exp", None),
        P("exp", "req"),
        P("req", "exp", None),
        P("exp", "req", None),
        P("exp", None),
        P("req", None),
        P(),
        P("exp", None),
        P("exp", None),
        P("exp", None, "req"),
        P("exp", None, "req"),
        P("exp", "req", None),
        P(None, "req"),
        P(None, "req"),
        P("req", None),
    )
    return jax.shard_map(
        on_device, mesh=mesh, in_specs=placed, out_specs=P("exp", None), check_vma=False
    )
```
